32 devices in a mesh: grp: 4 (over y, x), leaf: 8 (over z, core).
Axes of the slice: x: 2, y: 2, z: 4, core: 2. Of those that a mesh axis runs over, the one named last changes fastest.
Arguments:
- direction: bfloat16 [49152, 256], P(('grp', 'leaf')), may hold values from -6 to 6
- residual: bfloat16 [49152, 256], P(('grp', 'leaf')), may hold values from -6 to 6
- leaf_order: int32 [32, 1536], P(('grp', 'leaf')), may hold values from 0 to 1535, as said below
- diag_block: bfloat16 [32, 1536, 1536], P(('grp', 'leaf')), may hold values from -0.15625 to 0.15625
- up_basis: bfloat16 [32, 1536, 128], P(('grp', 'leaf')), may hold values from -0.15625 to 0.15625
- down_basis: bfloat16 [32, 1536, 128], P(('grp', 'leaf')), may hold values from -0.5 to 0.5
- leaf_ops: bfloat16 [3, 32, 128, 128], P(None, ('grp', 'leaf')), may hold values from -0.375 to 0.375
- inner_ops: bfloat16 [3, 24, 128, 128], P(None, 'grp'), may hold values from -0.375 to 0.375
- top_ops: bfloat16 [3, 6, 128, 128], replicated, may hold values from -0.375 to 0.375
- ridge_shift: float32 [1], replicated, may hold values from 0.5 to 2
Outputs:
- image: bfloat16 [49152, 256], P(('grp', 'leaf'))
- curvature_gram: float32 [256, 256], replicated
- residual_gram: float32 [256, 256], replicated
The draws below stay inside these ranges and needn't reach their ends.
Inputs may be any that keep to these rules, and one draw needn't show every extreme that they name: Each row of leaf_order is a permutation of 0 to 1535.
All inputs are finite; a program needn't handle non-finite values.
Results may differ from the reference program's by a relative error of at most 0.022.
Values may be sent and summed in bfloat16 or wider, within the bound.
No kernel may reach another device: no remote copies, remote signals or barrier semaphores. Data moves between devices by JAX's collectives and lax.ppermute only.
A program may use at most 64 MiB of HBM per device.

```python
import math
import jax
import jax.numpy as jnp
from jax import lax

LEAF = 1536
RANK = 128
NRHS = 256
LEAVES = 32
POINTS = 49152
INNER = 24
UPPER = 6
N_GRP = 4
N_LEAF = 8


def draw_leaf_order(key, part):
    row_keys = jax.random.split(jax.random.fold_in(key, 17), LEAVES)
    return jax.vmap(lambda single: jax.random.permutation(single, LEAF))(row_keys).astype(jnp.int32)


def block_levels(stream_key, shape, shards, low, top_value):
    loudness, own = 1.0, jax.random.fold_in(stream_key, 6)
    for position, shards_of in shards:
        steps = jnp.exp(jax.random.uniform(jax.random.fold_in(own, position), (shards_of,), jnp.float32, low / len(shards), top_value / len(shards)))
        loudness = loudness * jnp.repeat(steps, shape[position] // shards_of).reshape([-1 if axis == position else 1 for axis in range(len(shape))])
    return loudness


def centred(own_key, dims, scale, bound, cuts=(), kind=jnp.bfloat16):
    gain = block_levels(own_key, dims, cuts, -0.22, 0.18) if cuts else 1.0
    drawn = jax.random.normal(own_key, dims, jnp.float32) * scale * gain
    return jnp.minimum(jnp.maximum(drawn, -bound), bound).astype(kind)


def setup_inputs(seed: int = 0) -> dict:
    keys = jax.random.split(jax.random.key(seed), 11)
    direction = centred(keys[0], (POINTS, NRHS), 1.0, 6.0, ((0, 32),))
    residual = centred(keys[1], (POINTS, NRHS), 1.0, 6.0, ((0, 32),))
    leaf_order = draw_leaf_order(jax.random.fold_in(keys[10], 71), 0)
    diag_block = centred(keys[3], (LEAVES, LEAF, LEAF), LEAF ** -0.5, 0.15625, ((0, 32),))
    up_basis = centred(keys[4], (LEAVES, LEAF, RANK), LEAF ** -0.5, 0.15625, ((0, 32),))
    down_basis = centred(keys[5], (LEAVES, LEAF, RANK), RANK ** -0.5, 0.5, ((0, 32),))
    leaf_ops = centred(keys[6], (3, LEAVES, RANK, RANK), (2 * RANK) ** -0.5, 0.375, ((1, 32),))
    inner_ops = centred(keys[7], (3, INNER, RANK, RANK), (2 * RANK) ** -0.5, 0.375, ((1, 4),))
    top_ops = centred(keys[8], (3, UPPER, RANK, RANK), (2 * RANK) ** -0.5, 0.375)
    ridge_shift = jnp.clip(jnp.exp(jax.random.uniform(keys[9], (1,), jnp.float32, math.log(0.5), math.log(2.0))), 0.5, 2.0)
    return {"direction": direction, "residual": residual, "leaf_order": leaf_order, "diag_block": diag_block, "up_basis": up_basis, "down_basis": down_basis, "leaf_ops": leaf_ops, "inner_ops": inner_ops, "top_ops": top_ops, "ridge_shift": ridge_shift}


def level_operators(height, leaf_ops, inner_ops, top_ops):
    leaf_levels = N_LEAF.bit_length() - 1
    if height == 0:
        return leaf_ops
    if height < leaf_levels:
        offset = sum(N_LEAF >> section for section in range(1, height))
        node_count = N_LEAF >> height
        grouped = inner_ops.reshape(3, N_GRP, N_LEAF - 2, RANK, RANK)
        return grouped[:, :, offset:offset + node_count].reshape(3, N_GRP * node_count, RANK, RANK)
    upper_level = height - leaf_levels
    offset = sum(N_GRP >> section for section in range(upper_level))
    return top_ops[:, offset:offset + (N_GRP >> upper_level)]


def contribute(transfer, skeletons):
    product = jnp.einsum("nrs,nrk->nsk", transfer.astype(jnp.float32), skeletons.astype(jnp.float32))
    return product.astype(jnp.bfloat16)


def pair_sum(lifted):
    shaped = lifted.astype(jnp.float32).reshape(-1, 2, lifted.shape[1], lifted.shape[2])
    return (shaped[:, 0] + shaped[:, 1]).astype(jnp.bfloat16)


def project_up(pieces):
    return jnp.dot(pieces[0].T, pieces[1], preferred_element_type=jnp.float32).astype(jnp.bfloat16)


def leaf_apply(pieces):
    dense = jnp.dot(pieces[0], pieces[1], preferred_element_type=jnp.float32)
    return dense + jnp.dot(pieces[2], pieces[3], preferred_element_type=jnp.float32)


def reference(direction, residual, leaf_order, diag_block, up_basis, down_basis, leaf_ops, inner_ops, top_ops, ridge_shift):
    total_levels = (N_LEAF.bit_length() - 1) + (N_GRP.bit_length() - 1)
    blocks = direction.reshape(LEAVES, LEAF, NRHS)
    ordered = jnp.take_along_axis(blocks, leaf_order[:, :, None], axis=1)
    skeleton = lax.map(project_up, (up_basis, ordered))
    level_skeletons = [skeleton]
    for height in range(total_levels):
        operators = level_operators(height, leaf_ops, inner_ops, top_ops)
        skeleton = pair_sum(contribute(operators[0], skeleton))
        level_skeletons.append(skeleton)
    coarse = jnp.zeros((1, RANK, NRHS), jnp.bfloat16)
    for height in reversed(range(total_levels)):
        operators = level_operators(height, leaf_ops, inner_ops, top_ops)
        below = level_skeletons[height]
        sibling = jnp.flip(below.reshape(-1, 2, RANK, NRHS), axis=1).reshape(below.shape)
        parent = jnp.repeat(coarse, 2, axis=0)
        coupled = jnp.einsum("nrs,nsk->nrk", operators[2].astype(jnp.float32), sibling.astype(jnp.float32))
        passed = jnp.einsum("nrs,nsk->nrk", operators[1].astype(jnp.float32), parent.astype(jnp.float32))
        coarse = (coupled + passed).astype(jnp.bfloat16)
    local = lax.map(leaf_apply, (diag_block, ordered, down_basis, coarse))
    row_index = jnp.arange(LEAVES, dtype=jnp.int32)[:, None]
    restored = jnp.zeros_like(local).at[row_index, leaf_order].set(local)
    image = (restored.reshape(POINTS, NRHS) + ridge_shift[0] * direction.astype(jnp.float32)).astype(jnp.bfloat16)
    curvature = jnp.dot(direction.T, image, preferred_element_type=jnp.float32) / POINTS
    correlation = jnp.dot(residual.T, image, preferred_element_type=jnp.float32) / POINTS
    return (image, curvature, correlation)
```

```python
import jax
import jax.numpy as jnp
from jax import lax
from jax.sharding import PartitionSpec as P

BF = jnp.bfloat16
F32 = jnp.float32


def swap(block, axis, apart):
    count = lax.axis_size(axis)
    return lax.ppermute(block, axis, [(i, i ^ (1 << apart)) for i in range(count)])


def mm(a, b):
    return lax.dot_general(a, b, (((1,), (0,)), ((), ())), preferred_element_type=F32)


def mmt(a, b):
    return lax.dot_general(a, b, (((1,), (1,)), ((), ())), preferred_element_type=F32)


def cut(x, which, size, axis=0):
    return lax.dynamic_slice_in_dim(x, which * size, size, axis)


def join(bit, own, other, axis=0):
    low = jnp.where(bit == 0, own, other)
    high = jnp.where(bit == 0, other, own)
    return jnp.concatenate([low, high], axis)


def body(
    direction,
    residual,
    leaf_order,
    diag_block,
    up_basis,
    down_basis,
    leaf_ops,
    inner_ops,
    top_ops,
    ridge_shift,
):
    leaves_here = lax.axis_size("leaf")
    groups = lax.axis_size("grp")
    leaf_levels = leaves_here.bit_length() - 1
    group_levels = groups.bit_length() - 1
    total_levels = leaf_levels + group_levels
    my_leaf = lax.axis_index("leaf")
    my_group = lax.axis_index("grp")
    points, nrhs = direction.shape
    half = nrhs // 2
    core = my_leaf & 1
    ridge = ridge_shift[0]

    def node_ops(height, flip):
        if height < leaf_levels:
            start = sum(leaves_here >> s for s in range(1, height))
            node = start + ((my_leaf >> height) ^ flip)
            return lax.dynamic_index_in_dim(inner_ops, node, 1, keepdims=False)
        upper = height - leaf_levels
        start = sum(groups >> s for s in range(upper))
        node = start + ((my_group >> upper) ^ flip)
        return lax.dynamic_index_in_dim(top_ops, node, 1, keepdims=False)

    both = jnp.concatenate([direction, residual], 1)
    rows = lax.broadcasted_iota(jnp.int32, (points, points), 0)
    spread = (rows == leaf_order[0][None, :]).astype(BF)
    ordered = lax.dot_general(both, spread, (((0,), (0,)), ((), ())), preferred_element_type=F32).astype(BF)
    st = mm(ordered[:nrhs], up_basis[0]).astype(BF)
    vt = mm(ordered, down_basis[0]).astype(BF)
    up0, down0, cross0 = leaf_ops[0, 0], leaf_ops[1, 0], leaf_ops[2, 0]
    lift = mm(st, up0).astype(BF)
    vr = mm(vt, down0).astype(BF)
    vb = mm(vt, cross0).astype(BF)
    message = jnp.concatenate([st, cut(lift, 1 - core, half), vr, vb], 0)
    got = swap(message, "leaf", 0)
    dense = mmt(diag_block[0], ordered[:nrhs])
    gram = mm(ordered, dense.astype(BF)) + ridge * lax.dot_general(
        both, direction, (((0,), (0,)), ((), ())), preferred_element_type=F32
    )
    got_gram = swap(cut(gram, 1 - core, half, 1).astype(BF), "leaf", 0)
    leaf_sibling = got[:nrhs]
    got_lift = got[nrhs : nrhs + half]
    got_vr = got[nrhs + half : 3 * nrhs + half]
    got_vb = got[3 * nrhs + half :]
    s = (cut(lift, core, half).astype(F32) + got_lift.astype(F32)).astype(BF)
    v = (vr.astype(F32) + got_vr.astype(F32)).astype(BF)
    g = (
        cut(gram, core, half, 1)
        + got_gram.astype(F32)
        + (mmt(vb, cut(leaf_sibling, core, half)) + mmt(got_vb, cut(st, core, half)))
    )
    siblings = {}
    for height in range(1, total_levels):
        own_ops = node_ops(height, 0)
        sib_ops = node_ops(height, 1)
        scatter = height < leaf_levels
        if scatter:
            bit = (my_leaf >> height) & 1
            part = v.shape[0] // 2
            send_v, send_g = cut(v, 1 - bit, part), cut(g, 1 - bit, part).astype(BF)
            v, g = cut(v, bit, part), cut(g, bit, part)
            got = swap(jnp.concatenate([s, send_v, send_g], 0), "leaf", height)
        else:
            part = v.shape[0]
            send_g = g.astype(BF)
            g = send_g.astype(F32)
            got = swap(jnp.concatenate([s, v, send_g], 0), "grp", height - leaf_levels)
        s2, v2, g2 = got[:half], got[half : half + part], got[half + part :]
        siblings[height] = s2
        g = (g + g2.astype(F32)) + (
            mmt(mm(v, own_ops[2]).astype(BF), s2) + mmt(mm(v2, sib_ops[2]).astype(BF), s)
        )
        if height + 1 < total_levels:
            s = (mm(s, own_ops[0]) + mm(s2, sib_ops[0])).astype(BF)
            v = (mm(v, own_ops[1]) + mm(v2, sib_ops[1])).astype(BF)
    coarse = None
    for height in reversed(range(1, total_levels)):
        own_ops = node_ops(height, 0)
        term = mmt(siblings[height], own_ops[2])
        if coarse is not None:
            term = term + mmt(coarse, own_ops[1])
        coarse = term.astype(BF)
    coarse = join(core, coarse, swap(coarse, "leaf", 0))
    leaf_coarse = (mmt(leaf_sibling, cross0) + mmt(coarse, down0)).astype(BF)
    local = dense + mmt(down_basis[0], leaf_coarse)
    restored = mm(spread, local.astype(BF))
    image = (restored + ridge * direction.astype(F32)).astype(BF)
    piece = g.astype(BF)
    for height in reversed(range(1, leaf_levels)):
        piece = join((my_leaf >> height) & 1, piece, swap(piece, "leaf", height))
    piece = join(core, piece, swap(piece, "leaf", 0), 1)
    grams = piece.astype(F32) / (points * leaves_here * groups)
    return image, grams[:nrhs], grams[nrhs:]


def solution(mesh):
    return jax.shard_map(
        body,
        mesh=mesh,
        in_specs=(
            P(("grp", "leaf"), None),
            P(("grp", "leaf"), None),
            P(("grp", "leaf"), None),
            P(("grp", "leaf"), None, None),
            P(("grp", "leaf"), None, None),
            P(("grp", "leaf"), None, None),
            P(None, ("grp", "leaf"), None, None),
            P(None, "grp", None, None),
            P(),
            P(),
        ),
        out_specs=(P(("grp", "leaf"), None), P(), P()),
        check_vma=False,
    )
```

```python
import functools

import jax
import jax.numpy as jnp
from jax import lax
from jax.experimental import pallas as pl
from jax.experimental.pallas import tpu as pltpu
from jax.sharding import PartitionSpec as P

BF = jnp.bfloat16
F32 = jnp.float32
I16 = jnp.int16
MIB = 2**20
VM = pl.BlockSpec(memory_space=pltpu.VMEM)
SM = pl.BlockSpec(memory_space=pltpu.SMEM)
FAR = pl.BlockSpec(memory_space=pltpu.HBM)


def mm(a, b):
    return lax.dot_general(a, b, (((1,), (0,)), ((), ())), preferred_element_type=F32)


def mmt(a, b):
    return lax.dot_general(a, b, (((1,), (1,)), ((), ())), preferred_element_type=F32)


def shape(dims, kind=BF):
    return jax.ShapeDtypeStruct(dims, kind)


def cost(flops, moved):
    return pl.CostEstimate(flops=flops, bytes_accessed=moved, transcendentals=0)


def swap(block, axis, mask):
    count = lax.axis_size(axis)
    return lax.ppermute(block, axis, [(i, i ^ mask) for i in range(count)])


class Phase:
    def __init__(self, axis, first, bits, height, sizes):
        self.axis, self.first, self.bits, self.height = axis, first, bits, height
        self.parts = 1 << bits
        self.scatter = axis == "leaf"
        self.leaves, self.groups = sizes

    def index(self):
        return lax.axis_index(self.axis)

    def place(self):
        return (self.index() >> self.first) & (self.parts - 1)

    def node(self, level, j):
        bit = self.first + level
        if self.axis == "leaf":
            start = sum(self.leaves >> s for s in range(1, bit))
        else:
            start = sum(self.groups >> s for s in range(bit))
        return start + ((self.index() >> (self.first + self.bits)) << (self.bits - level)) + j


def plan(leaves, groups):
    phases = []
    leaf_levels, group_levels = leaves.bit_length() - 1, groups.bit_length() - 1
    for axis, low, high in (("leaf", 1, leaf_levels), ("grp", 0, group_levels)):
        bit = low
        while bit < high:
            bits = min(2, high - bit)
            height = bit if axis == "leaf" else leaf_levels + bit
            phases.append(Phase(axis, bit, bits, height, (leaves, groups)))
            bit += bits
    return phases


def front_kernel(chunk, ridge_ref, order_far, ops_far, d_far, r_far, diag_far, up_far, down_far,
                 msg_ref, keep_ref, gown_ref, dense_far,
                 order_v, ops_v, d_v, r_v, diag_v, up_v, down_v, bt, xt, dense_v, sems):
    points, nrhs = d_v.shape
    half = nrhs // 2
    n = points // chunk
    flip = (lax.axis_index("leaf") & 1) == 0

    def start(src, dst, i):
        copy = pltpu.make_async_copy(src, dst, sems.at[i])
        copy.start()
        return copy

    c_order = start(order_far, order_v, 0)
    c_d = start(d_far, d_v, 1)
    c_r = start(r_far, r_v, 2)
    c_up = start(up_far.at[0], up_v, 3)
    c_down = start(down_far.at[0], down_v, 4)
    c_ops = start(ops_far, ops_v, 5)
    c_order.wait()
    c_d.wait()
    c_diag = [
        start(diag_far.at[0, pl.ds(i * chunk, chunk)], diag_v.at[pl.ds(i * chunk, chunk)], 6 + i)
        for i in range(n)
    ]
    bt[:nrhs] = d_v[...].T
    c_r.wait()
    bt[nrhs:] = r_v[...].T
    rows = lax.broadcasted_iota(jnp.int32, (points, chunk), 0).astype(I16)

    def spread(i, carry):
        at = pl.ds(pl.multiple_of(i * chunk, chunk), chunk)
        hot = jnp.where(rows == order_v[:, at].astype(I16), BF(1), BF(0))
        xt[:, at] = mm(bt[...], hot).astype(BF)
        return carry

    lax.fori_loop(0, n, spread, 0)
    c_up.wait()
    c_down.wait()
    c_ops.wait()
    st = mm(xt[:nrhs], up_v[...]).astype(BF)
    vt = mm(xt[...], down_v[...]).astype(BF)
    lift = mm(st, ops_v[0, 0]).astype(BF)
    vr = mm(vt, ops_v[1, 0]).astype(BF)
    vb = mm(vt, ops_v[2, 0]).astype(BF)
    b = nrhs + half
    msg_ref[:nrhs] = st
    msg_ref[nrhs:b] = jnp.where(flip, lift[half:], lift[:half])
    msg_ref[b : b + 2 * nrhs] = vr
    msg_ref[b + 2 * nrhs : b + 4 * nrhs] = vb
    keep_ref[:half] = jnp.where(flip, st[:half], st[half:])
    keep_ref[half:nrhs] = jnp.where(flip, lift[:half], lift[half:])
    keep_ref[nrhs : 3 * nrhs] = vr
    keep_ref[3 * nrhs :] = vb
    c_out = []
    for i in range(n):
        c_diag[i].wait()
        at = pl.ds(i * chunk, chunk)
        dense_v[at] = mmt(diag_v[at], xt[:nrhs]).astype(BF)
        c_out.append(start(dense_v.at[at], dense_far.at[at], 6 + n + i))
    gram = mm(xt[...], dense_v[...]) + ridge_ref[0] * mm(bt[...], d_v[...])
    msg_ref[b + 4 * nrhs :] = jnp.where(flip, gram[:, half:], gram[:, :half]).astype(BF)
    gown_ref[...] = jnp.where(flip, gram[:, :half], gram[:, half:])
    for copy in c_out:
        copy.wait()


def front(ridge, order, ops, d, r, diag, up, down):
    points, nrhs = d.shape
    rank = up.shape[2]
    half = nrhs // 2
    chunk = points // 2 if points // 2 % 128 == 0 else points
    n = points // chunk
    return pl.pallas_call(
        functools.partial(front_kernel, chunk),
        out_shape=(
            shape((7 * nrhs + half, rank)),
            shape((5 * nrhs, rank)),
            shape((2 * nrhs, half), F32),
            shape((points, nrhs)),
        ),
        in_specs=[SM] + [FAR] * 7,
        out_specs=(VM, VM, VM, FAR),
        scratch_shapes=[
            pltpu.VMEM(order.shape, jnp.int32),
            pltpu.VMEM(ops.shape, BF),
            pltpu.VMEM((points, nrhs), BF),
            pltpu.VMEM((points, nrhs), BF),
            pltpu.VMEM((points, points), BF),
            pltpu.VMEM((points, rank), BF),
            pltpu.VMEM((points, rank), BF),
            pltpu.VMEM((2 * nrhs, points), BF),
            pltpu.VMEM((2 * nrhs, points), BF),
            pltpu.VMEM((points, nrhs), BF),
            pltpu.SemaphoreType.DMA((6 + 2 * n,)),
        ],
        compiler_params=pltpu.CompilerParams(vmem_limit_bytes=FRONT_LIMIT),
        cost_estimate=cost(5 * points * points * nrhs, 2 * points * points),
        name="front",
    )(ridge, order, ops, d, r, diag, up, down)


FRONT_LIMIT = 61 * MIB


def emit(phase, s, v, g, v_s, g_s, outs):
    if phase is None:
        outs[0][...] = g.astype(BF)
        return
    rank = s.shape[0]
    if not phase.scatter:
        rows = v.shape[0]
        outs[0][:rank] = s
        outs[0][rank : rank + rows] = v
        outs[0][rank + rows :] = g.astype(BF)
        return
    v_s[...] = v
    g_s[...] = g
    piece = v.shape[0] // phase.parts
    place = phase.place()
    for mask in range(1, phase.parts):
        at = pl.ds(pl.multiple_of((place ^ mask) * piece, piece), piece)
        outs[mask][:rank] = s
        outs[mask][rank : rank + piece] = v_s[at]
        outs[mask][rank + piece :] = g_s[at].astype(BF)
    at = pl.ds(pl.multiple_of(place * piece, piece), piece)
    outs[0][:rank] = s
    outs[0][rank:] = v_s[at]
    outs[-1][...] = g_s[at]


def emit_shapes(phase, cols, rows, rank):
    if phase is None:
        return [shape((rows, cols))]
    if not phase.scatter:
        return [shape((cols + 2 * rows, rank))]
    piece = rows // phase.parts
    return (
        [shape((cols + piece, rank))]
        + [shape((cols + 2 * piece, rank))] * (phase.parts - 1)
        + [shape((piece, cols), F32)]
    )


def core_kernel(phase, got, keep, gown, *rest):
    outs, (v_s, g_s) = rest[:-2], rest[-2:]
    half = gown.shape[1]
    nrhs = 2 * half
    flip = (lax.axis_index("leaf") & 1) == 0
    b = nrhs + half
    sib = jnp.where(flip, got[:half], got[half:nrhs])
    s = (keep[half:nrhs].astype(F32) + got[nrhs:b].astype(F32)).astype(BF)
    v = (keep[nrhs : 3 * nrhs].astype(F32) + got[b : b + 2 * nrhs].astype(F32)).astype(BF)
    g = (
        gown[...]
        + got[b + 4 * nrhs :].astype(F32)
        + (mmt(keep[3 * nrhs :], sib) + mmt(got[b + 2 * nrhs : b + 4 * nrhs], keep[:half]))
    )
    emit(phase, s, v, g, v_s, g_s, outs)


def core_merge(phase, got, keep, gown):
    rows, cols = gown.shape
    rank = keep.shape[1]
    return pl.pallas_call(
        functools.partial(core_kernel, phase),
        out_shape=tuple(emit_shapes(phase, cols, rows, rank)),
        in_specs=[VM] * 3,
        out_specs=tuple([VM] * len(emit_shapes(phase, cols, rows, rank))),
        scratch_shapes=[pltpu.VMEM((rows, rank), BF), pltpu.VMEM((rows, cols), F32)],
        compiler_params=pltpu.CompilerParams(vmem_limit_bytes=8 * MIB),
        cost_estimate=cost(4 * rows * cols * rank, 4 * rows * rank),
        name="core_merge",
    )(got, keep, gown)


def merge_kernel(phase, following, last, own, gots, gown, ops, outs, scratch):
    v_s, g_s, s_in, v_in, g_in, levels = scratch
    cols, rank = s_in.shape[1:]
    rows = v_in.shape[1]
    place = phase.place()
    blocks = [(place, own)] + [(place ^ (m + 1), got) for m, got in enumerate(gots)]
    for slot, block in blocks:
        s_in[slot] = block[:cols]
        v_in[slot] = block[cols : cols + rows]
        if not phase.scatter:
            g_in[slot] = block[cols + rows :]
    if phase.scatter:
        g = gown[...]
        for got in gots:
            g = g + got[cols + rows :].astype(F32)
    else:
        g = g_in[0].astype(F32)
        for j in range(1, phase.parts):
            g = g + g_in[j].astype(F32)
    s = [s_in[j] for j in range(phase.parts)]
    v = [v_in[j] for j in range(phase.parts)]
    sib_out = outs[-1]
    for level in range(phase.bits):
        for j, block in enumerate(s):
            levels[j] = block
        sib_out[level] = levels[(place >> level) ^ 1]
        at = [phase.node(level, j) for j in range(len(s))]
        up_s, up_v = [], []
        for a in range(0, len(s), 2):
            c = a + 1
            va = mm(v[a], ops[2, at[a]]).astype(BF)
            vc = mm(v[c], ops[2, at[c]]).astype(BF)
            g = g + (mmt(va, s[c]) + mmt(vc, s[a]))
            if not (last and level == phase.bits - 1):
                up_s.append((mm(s[a], ops[0, at[a]]) + mm(s[c], ops[0, at[c]])).astype(BF))
                up_v.append((mm(v[a], ops[1, at[a]]) + mm(v[c], ops[1, at[c]])).astype(BF))
        s, v = up_s, up_v
    emit(following, s[0] if s else None, v[0] if v else None, g, v_s, g_s, outs[:-1])


def merge(phase, following, own, gots, gown, ops, cols):
    rank = own.shape[1]
    rows = gots[0].shape[0] // 2 - cols // 2
    outs = emit_shapes(following, cols, rows, rank) + [shape((phase.bits, cols, rank))]
    args = [own, *gots] + ([gown] if phase.scatter else []) + [ops]

    def kernel(*refs):
        ins, rest = refs[: len(args)], refs[len(args) :]
        merge_kernel(
            phase,
            following,
            following is None,
            ins[0],
            ins[1 : phase.parts],
            ins[phase.parts] if phase.scatter else None,
            ins[-1],
            rest[: len(outs)],
            rest[len(outs) :],
        )

    return pl.pallas_call(
        kernel,
        out_shape=tuple(outs),
        in_specs=[VM] * len(args),
        out_specs=tuple([VM] * len(outs)),
        scratch_shapes=[
            pltpu.VMEM((rows, rank), BF),
            pltpu.VMEM((rows, cols), F32),
            pltpu.VMEM((phase.parts, cols, rank), BF),
            pltpu.VMEM((phase.parts, rows, rank), BF),
            pltpu.VMEM((phase.parts, rows, cols), BF),
            pltpu.VMEM((phase.parts, cols, rank), BF),
        ],
        compiler_params=pltpu.CompilerParams(vmem_limit_bytes=8 * MIB),
        cost_estimate=cost(40 * rows * cols * rank, 20 * rows * rank),
        name=f"merge_{phase.axis}{phase.first}",
    )(*args)


def down_kernel(phases, *refs):
    sibs, (inner, top, out) = refs[: len(phases)], refs[len(phases) :]
    coarse = None
    for phase, sib in reversed(list(zip(phases, sibs))):
        ops = inner if phase.axis == "leaf" else top
        for level in reversed(range(phase.bits)):
            at = phase.node(level, phase.place() >> level)
            term = mmt(sib[level], ops[2, at])
            if coarse is not None:
                term = term + mmt(coarse, ops[1, at])
            coarse = term.astype(BF)
    out[...] = coarse


def down_pass(phases, sibs, inner, top):
    cols, rank = sibs[0].shape[1:]
    return pl.pallas_call(
        functools.partial(down_kernel, phases),
        out_shape=shape((cols, rank)),
        in_specs=[VM] * (len(sibs) + 2),
        out_specs=VM,
        compiler_params=pltpu.CompilerParams(vmem_limit_bytes=8 * MIB),
        cost_estimate=cost(20 * cols * rank * rank, 20 * cols * rank),
        name="down_pass",
    )(*sibs, inner, top)


def image_kernel(chunk, ridge_ref, order, own, other, got, ops, down, dense, d, out, local):
    points, nrhs = d.shape
    half = own.shape[0]
    flip = (lax.axis_index("leaf") & 1) == 0
    low = jnp.where(flip, own[...], other[...])
    high = jnp.where(flip, other[...], own[...])
    parent = jnp.concatenate([low, high], 0)
    coarse = (mmt(got[:nrhs], ops[2, 0]) + mmt(parent, ops[1, 0])).astype(BF)
    local[...] = (dense[...].astype(F32) + mmt(down[0], coarse)).astype(BF)
    to = order[...].astype(I16)

    def place(i, carry):
        at = pl.ds(pl.multiple_of(i * chunk, chunk), chunk)
        rows = (lax.broadcasted_iota(jnp.int32, (chunk, points), 0) + i * chunk).astype(I16)
        hot = jnp.where(rows == to, BF(1), BF(0))
        out[at] = (mm(hot, local[...]) + ridge_ref[0] * d[at].astype(F32)).astype(BF)
        return carry

    lax.fori_loop(0, points // chunk, place, 0)


def image_of(ridge, order, own, other, got, ops, down, dense, d):
    points, nrhs = d.shape
    chunk = points // 3 if points % 384 == 0 else points
    return pl.pallas_call(
        functools.partial(image_kernel, chunk),
        out_shape=shape((points, nrhs)),
        in_specs=[SM] + [VM] * 8,
        out_specs=VM,
        scratch_shapes=[pltpu.VMEM((points, nrhs), BF)],
        compiler_params=pltpu.CompilerParams(vmem_limit_bytes=24 * MIB),
        cost_estimate=cost(2 * points * points * nrhs, 6 * points * nrhs),
        name="image",
    )(ridge, order, own, other, got, ops, down, dense, d)


def join_kernel(phase, *refs):
    out = refs[-1]
    rows = refs[0].shape[0]
    place = phase.place()
    for mask in range(phase.parts):
        out[pl.ds(pl.multiple_of((place ^ mask) * rows, rows), rows)] = refs[mask][...]


def join(phase, pieces):
    rows, cols = pieces[0].shape
    return pl.pallas_call(
        functools.partial(join_kernel, phase),
        out_shape=shape((rows * phase.parts, cols)),
        in_specs=[VM] * phase.parts,
        out_specs=VM,
        compiler_params=pltpu.CompilerParams(vmem_limit_bytes=4 * MIB),
        name="join",
    )(*pieces)


def finish_kernel(total, own, other, first, second):
    half = own.shape[1]
    nrhs = 2 * half
    flip = (lax.axis_index("leaf") & 1) == 0
    low = jnp.where(flip, own[...], other[...]).astype(F32) / total
    high = jnp.where(flip, other[...], own[...]).astype(F32) / total
    first[:, :half] = low[:nrhs]
    first[:, half:] = high[:nrhs]
    second[:, :half] = low[nrhs:]
    second[:, half:] = high[nrhs:]


def finish(total, own, other):
    rows, half = own.shape
    return pl.pallas_call(
        functools.partial(finish_kernel, total),
        out_shape=(shape((rows // 2, 2 * half), F32), shape((rows // 2, 2 * half), F32)),
        in_specs=[VM] * 2,
        out_specs=(VM, VM),
        compiler_params=pltpu.CompilerParams(vmem_limit_bytes=4 * MIB),
        name="finish",
    )(own, other)


def body(
    direction,
    residual,
    leaf_order,
    diag_block,
    up_basis,
    down_basis,
    leaf_ops,
    inner_ops,
    top_ops,
    ridge_shift,
):
    leaves, groups = lax.axis_size("leaf"), lax.axis_size("grp")
    phases = plan(leaves, groups)
    points, nrhs = direction.shape
    half = nrhs // 2
    message, keep, gown, dense = front(
        ridge_shift, leaf_order, leaf_ops, direction, residual, diag_block, up_basis, down_basis
    )
    got0 = swap(message, "leaf", 1)
    sent = core_merge(phases[0], got0, keep, gown)
    sibs = []
    for i, phase in enumerate(phases):
        following = phases[i + 1] if i + 1 < len(phases) else None
        masks = range(1, phase.parts)
        out = [sent[m] if phase.scatter else sent[0] for m in masks]
        gots = [swap(out[m - 1], phase.axis, m << phase.first) for m in masks]
        *sent, sib = merge(
            phase,
            following,
            sent[0],
            gots,
            sent[-1] if phase.scatter else None,
            inner_ops if phase.axis == "leaf" else top_ops,
            half,
        )
        sibs.append(sib)
    piece = sent[0]
    coarse = down_pass(phases, sibs, inner_ops, top_ops)
    coarse_other = swap(coarse, "leaf", 1)
    image = image_of(
        ridge_shift, leaf_order, coarse, coarse_other, got0, leaf_ops, down_basis, dense, direction
    )
    for phase in reversed(phases):
        if phase.scatter:
            gots = [swap(piece, "leaf", m << phase.first) for m in range(1, phase.parts)]
            piece = join(phase, [piece, *gots])
    other = swap(piece, "leaf", 1)
    curvature, correlation = finish(points * leaves * groups, piece, other)
    return image, curvature, correlation


def solution(mesh):
    return jax.shard_map(
        body,
        mesh=mesh,
        in_specs=(
            P(("grp", "leaf"), None),
            P(("grp", "leaf"), None),
            P(("grp", "leaf"), None),
            P(("grp", "leaf"), None, None),
            P(("grp", "leaf"), None, None),
            P(("grp", "leaf"), None, None),
            P(None, ("grp", "leaf"), None, None),
            P(None, "grp", None, None),
            P(),
            P(),
        ),
        out_specs=(P(("grp", "leaf"), None), P(), P()),
        check_vma=False,
    )
```
